32 devices in a mesh: layer: 2 (over x), trow: 2 (over y), tcol: 8 (over z, core).
Axes of the slice: x: 2, y: 2, z: 4, core: 2. Of those that a mesh axis runs over, the one named last changes fastest.
Arguments:
- act_rows: bfloat16 [2, 1024, 4096], P('layer', ('trow', 'tcol')), may hold values from -6 to 6
- back_rows: bfloat16 [2, 1024, 4096], P('layer', ('trow', 'tcol')), may hold values from -6 to 6
- act_cols: bfloat16 [2, 2048, 4096], P('layer', ('tcol', 'trow')), may hold values from -6 to 6
- back_cols: bfloat16 [2, 2048, 4096], P('layer', ('tcol', 'trow')), may hold values from -6 to 6
Outputs:
- kernel: float32 [1024, 2048], P(('trow', 'layer'), 'tcol')
The draws below stay inside these ranges and needn't reach their ends.
All inputs are finite; a program needn't handle non-finite values.
Results may differ from the reference program's by a relative error of at most 0.0003.
Values may be sent and summed in bfloat16 or wider, within the bound.
A program may use at most 64 MiB of HBM per device.

```python
import jax
import jax.numpy as jnp

D = 4096
LAYERS = 2
ROWS = 1024
COLS = 2048


def shard_levels(rng, extent, pieces, smallest, high):
    def one(position, blocks):
        heights = jax.random.uniform(jax.random.fold_in(jax.random.fold_in(rng, 6), position), (blocks,), jnp.float32, smallest / len(pieces), high / len(pieces))
        return jnp.repeat(jnp.exp(heights), extent[position] // blocks).reshape((-1,) + (1,) * (len(extent) - position - 1))

    loudness = one(*pieces[0])
    for cut in pieces[1:]:
        loudness = loudness * one(*cut)
    return loudness


def scatter_about(key, dims, scale, bound, cuts=(), held_as=jnp.bfloat16):
    entries = jax.random.normal(key, dims, jnp.float32) * scale
    if len(cuts) > 0:
        entries = shard_levels(key, dims, cuts, -0.22, 0.18) * entries
    return jnp.clip(entries, min=-bound, max=bound).astype(held_as)


def setup_inputs(seed: int = 0) -> dict:
    streams_of = jax.random.split(jax.random.key(seed), 5)
    act_rows = scatter_about(streams_of[0], (LAYERS, ROWS, D), 1.0, 6.0, ((0, 2), (1, 16)))
    back_rows = scatter_about(streams_of[1], (LAYERS, ROWS, D), 1.0, 6.0, ((0, 2), (1, 16)))
    act_cols = scatter_about(streams_of[2], (LAYERS, COLS, D), 1.0, 6.0, ((0, 2), (1, 16)))
    back_cols = scatter_about(streams_of[3], (LAYERS, COLS, D), 1.0, 6.0, ((0, 2), (1, 16)))
    return dict(act_rows=act_rows, back_rows=back_rows, act_cols=act_cols, back_cols=back_cols)


def reference(act_rows, back_rows, act_cols, back_cols):
    total = jnp.zeros((ROWS, COLS), jnp.float32)
    for index in range(LAYERS):
        gram_act = jnp.dot(act_rows[index], act_cols[index].T, preferred_element_type=jnp.float32)
        gram_back = jnp.dot(back_rows[index], back_cols[index].T, preferred_element_type=jnp.float32)
        total = total + gram_act * gram_back
    return total / D
```

```python
import functools

import jax
import jax.numpy as jnp
from jax import lax
from jax.experimental import pallas as pl
from jax.experimental.pallas import tpu as pltpu
from jax.sharding import PartitionSpec as P

MESH = pl.DeviceIdType.MESH
CORES = 2
GRANULE = 16
AHEAD = 2
TRANS = (((1,), (1,)), ((), ()))


def kernel(sizes, act_rows, back_rows, act_cols, back_cols, out, rows, cols, far, term, got, made, given,
           own_sem, row_recv, mate_recv, in_send, out_send, pair_send, col_send, col_recv, far_send, far_recv,
           made_send, given_recv, term_send, term_recv):
    layers, trows, tcols, pieces, cut, kept = sizes
    depth = tcols // CORES
    per = depth // layers
    held, width = act_rows.shape[1:]
    part = held // pieces
    block = CORES * held
    strip = act_cols.shape[1]
    lay, trow, me = lax.axis_index("layer"), lax.axis_index("trow"), lax.axis_index("tcol")
    z, core = me // CORES, me % CORES
    mate, other = z * CORES + 1 - core, 1 - trow
    own_rows, own_cols = (act_rows, back_rows), (act_cols, back_cols)
    chunks = [(a, h) for h in range(pieces) for a in range(2)]
    low = z < depth // 2
    way = jnp.where(low, 1, -1)
    n_in = jnp.where(low, depth - 1 - z, z)
    n_out = depth - 1 - n_in
    edge, inner, middle = n_out == 0, n_out == 1, n_out > 1
    inwards, outwards = me + way * CORES, me - way * CORES

    own = []
    for a in range(2):
        mine = rows.at[a, pl.ds(pl.multiple_of(me * held, held), held)]
        own.append(pltpu.make_async_copy(own_rows[a].at[0], mine, own_sem.at[a]))
        strips = cols.at[a, pl.ds(pl.multiple_of(trow * strip, strip), strip)]
        own.append(pltpu.make_async_copy(own_cols[a].at[0], strips, own_sem.at[2 + a]))

    barrier = pltpu.get_barrier_semaphore()

    def greet(device):
        pl.semaphore_signal(barrier, inc=1, device_id=device, device_id_type=MESH)

    greet({"trow": other})
    greet({"tcol": inwards})

    @pl.when(~edge)
    def _():
        greet({"tcol": outwards})

    for step in range(1, layers):
        greet({"layer": lax.rem(lay + step, layers)})
    greet({"tcol": mate})
    for copy in own:
        copy.start()
    pl.semaphore_wait(barrier, layers + 2 + jnp.minimum(n_out, 1))

    def remote(src, dst, send, recv, device):
        return pltpu.make_async_remote_copy(
            src_ref=src, dst_ref=dst, send_sem=send, recv_sem=recv, device_id=device, device_id_type=MESH
        )

    def arrival(ref, sem):
        pltpu.make_async_copy(ref, ref, sem).wait()


    def row_block(origin, a, h, narrow):
        span = pl.ds(pl.multiple_of(origin * held + h * part, part), part)
        return rows.at[a, span, pl.ds(0, kept)] if narrow else rows.at[a, span]

    def row_copy(origin, a, h, mine, send, recv, target, narrow):
        dst = row_block(origin, a, h, narrow)
        src = dst
        if mine:
            span = pl.ds(h * part, part)
            src = own_rows[a].at[0, span, pl.ds(0, kept)] if narrow else own_rows[a].at[0, span]
        return remote(src, dst, send.at[origin, a], recv, {"tcol": target})

    def chain_recv(origin, a, h):
        return row_recv.at[origin, a * pieces + h]

    def either(a, narrow, body):
        if a == 0:
            body(False)
        else:
            pl.when(~narrow)(lambda: body(False))
            pl.when(narrow)(lambda: body(True))

    def send_in(origin, a, h, mine):
        row_copy(origin, a, h, mine, in_send, chain_recv(origin, a, h), inwards, False).start()

    def send_out(origin, a, h, mine):
        either(a, inner, lambda narrow: row_copy(
            origin, a, h, mine, out_send, chain_recv(origin, a, h), outwards, narrow).start())

    def send_pair(origin, a, h, mine):
        def send(narrow):
            row_copy(origin, a, h, mine, pair_send, mate_recv.at[origin, a], mate, narrow).start()

        if mine:
            send(False)
        else:
            either(a, edge, send)

    def row_arrival(origin, a, h):
        either(a, edge, lambda narrow: arrival(row_block(origin, a, h, narrow), chain_recv(origin, a, h)))

    def held_block(origin, a, narrow):
        mine = pl.ds(pl.multiple_of(origin * held, held), held)
        return rows.at[a, mine, pl.ds(0, kept)] if narrow else rows.at[a, mine]

    def from_mate(chip):
        origin = chip * CORES + 1 - core
        for a in range(2):
            either(a, edge & (chip != z),
                   lambda narrow: arrival(held_block(origin, a, narrow), mate_recv.at[origin, a]))


    lengths = (cut, strip - cut)

    def span(t, p):
        return pl.ds(pl.multiple_of(t * strip + p * cut, GRANULE), lengths[p])

    def strip_of(t):
        return pl.ds(pl.multiple_of(t * strip, strip), strip)

    def col_copy(a, p, start=0, stop=width, sem=None):
        sem = a if sem is None else sem
        src = own_cols[a].at[0, pl.ds(p * cut, lengths[p]), pl.ds(start, stop - start)]
        dst = cols.at[a, span(trow, p), pl.ds(start, stop - start)]
        return remote(src, dst, col_send.at[sem, p], col_recv.at[sem, p], {"trow": other})

    def col_arrival(a, p, start=0, stop=width, sem=None):
        sem = a if sem is None else sem
        arrival(cols.at[a, span(other, p), pl.ds(start, stop - start)], col_recv.at[sem, p])

    def edge_cols():
        return [col_copy(1, 1, kept, width, 2), col_copy(0, 0), col_copy(0, 1), col_copy(1, 0),
                col_copy(1, 1, 0, kept)]

    def inner_cols():
        return [col_copy(0, 0), col_copy(0, 1), col_copy(1, 0), col_copy(1, 1)]

    def far_own(p):
        src = back_cols.at[0, pl.ds(p * cut, lengths[p]), pl.ds(kept, width - kept)]
        return remote(src, far.at[span(trow, p)], far_send.at[p], far_recv.at[trow, p], {"tcol": inwards})

    def far_inward():
        src = cols.at[1, span(other, 1), pl.ds(kept, width - kept)]
        return remote(src, far.at[span(other, 1)], far_send.at[2], far_recv.at[other, 1], {"tcol": inwards})

    def far_across():
        held_far = far.at[span(trow, 0)]
        return remote(held_far, held_far, far_send.at[3], far_recv.at[trow, 0], {"trow": other})

    def far_arrival(t, p):
        arrival(far.at[span(t, p)], far_recv.at[t, p])


    def made_copy(chip, t, p):
        return remote(made.at[chip, span(t, p)], given.at[chip, span(t, p)], made_send.at[chip, t, p],
                      given_recv.at[chip, t, p], {"tcol": outwards})

    def term_copy(chip, t, p):
        j, d = lax.rem(chip, per), chip // per
        return remote(term.at[chip, span(t, p)], got.at[lay, j, span(t, p)], term_send.at[chip, t, p],
                      term_recv.at[lay, j, t, p], {"layer": d})

    def send_term(chip, t, p):
        @pl.when(chip // per != lay)
        def _():
            term_copy(chip, t, p).start()

    def rows_of(a, chip, start, stop):
        return rows[a, pl.ds(pl.multiple_of(chip * block, block), block), start:stop]

    def gram(left, a, chip, start=0, stop=width):
        return lax.dot_general(left, rows_of(a, chip, start, stop), TRANS, preferred_element_type=jnp.float32)

    def act(chip, where):
        term[chip, where, :] = gram(cols[0, where, :], 0, chip)

    def back(chip, where):
        term[chip, where, :] = term[chip, where, :] * gram(cols[1, where, :], 1, chip)

    def near(chip, where):
        made[chip, where, :] = gram(cols[1, where, :kept], 1, chip, 0, kept)

    def make_far(chip, t, p):
        where = span(t, p)
        made[chip, where, :] = gram(far[where, :], 1, chip, kept)
        made_copy(chip, t, p).start()

    def use_given(chip, t, p):
        where = span(t, p)
        arrival(given.at[chip, where], given_recv.at[chip, t, p])
        term[chip, where, :] = term[chip, where, :] * (made[chip, where, :] + given[chip, where, :])
        send_term(chip, t, p)

    def send_strip(chip, t):
        for p in range(2):
            send_term(chip, t, p)

    def inward_chip(hop):
        return z + way * hop

    def late_chip(i):
        hop = i + 2
        return jnp.where(hop <= n_in, z + way * hop, z - way * (hop - n_in))

    def loop(count, body):
        def step(i, carry):
            body(i)
            return carry

        lax.fori_loop(0, count, step, 0)


    @pl.when(edge)
    def _():
        for p in range(2):
            far_own(p).start()
        for copy in edge_cols():
            copy.start()

    for a, h in chunks:
        send_in(me, a, h, True)

        @pl.when(~edge)
        def _():
            send_out(me, a, h, True)

    @pl.when(~edge)
    def _():
        inner_cols()[0].start()

    @pl.when(middle)
    def _():
        for copy in inner_cols()[1:]:
            copy.start()

    for a, h in chunks:
        send_pair(me, a, h, True)


    def pass_out(origin, a, h):
        row_arrival(origin, a, h)

        @pl.when(~edge)
        def _():
            send_out(origin, a, h, False)

        send_pair(origin, a, h, False)

    def pass_in(origin, a, h):
        row_arrival(origin, a, h)
        send_in(origin, a, h, False)
        send_pair(origin, a, h, False)

    def edge_chunk(a, h):
        @pl.when(inner)
        def _():
            pass_in(me - way * CORES, a, h)

    def chunk(slot, a, h):
        @pl.when(n_in >= slot)
        def _():
            pass_out(me + way * slot * CORES, a, h)

        @pl.when(n_out >= max(slot, 2))
        def _():
            if slot == 1:
                pass_in(me - way * CORES, a, h)
            else:
                pass_in(me - way * slot * CORES, a, h)

    last = len(chunks) - 1
    mine, theirs = strip_of(trow), strip_of(other)
    chip_in = inward_chip(1)

    def hook(slot, i):
        if slot == 1 and i == min(2, last):
            @pl.when(inner)
            def _():
                far_arrival(trow, 0)
                far_across().start()
                for copy in inner_cols()[1:]:
                    copy.start()

        if slot == 1 and i == min(4, last):
            @pl.when(edge)
            def _():
                col_arrival(1, 1, kept, width, 2)
                far_inward().start()

        if slot == 1 and i == last:
            for copy in own:
                copy.wait()
            from_mate(z)
            from_mate(chip_in)

            @pl.when(inner)
            def _():
                far_arrival(trow, 1)
                for p in range(2):
                    make_far(z, trow, p)
                    make_far(chip_in, trow, p)
                far_arrival(other, 0)
                make_far(z, other, 0)
                make_far(chip_in, other, 0)

        if slot == 2 and i == min(1, last):
            act(z, mine)
            act(chip_in, mine)

            @pl.when(~edge)
            def _():
                back(z, mine)
                back(chip_in, mine)
                send_strip(z, trow)
                send_strip(chip_in, trow)

            @pl.when(edge)
            def _():
                back(z, mine)
                near(chip_in, mine)
                send_strip(z, trow)

        if slot == 2 and i == min(4, last):
            for p in range(2):
                col_arrival(0, p)
            act(z, theirs)
            act(chip_in, theirs)

    for slot in range(1, depth):
        for i, (a, h) in enumerate(chunks):
            early = i + AHEAD if slot == 2 else i + AHEAD - len(chunks)
            if slot <= 2 and 0 <= early <= last:
                edge_chunk(*chunks[early])

            chunk(slot, a, h)
            hook(slot, i)

    loop(depth - 2, lambda i: from_mate(late_chip(i)))

    @pl.when(inner)
    def _():
        def late(i):
            chip = late_chip(i)
            for p in range(2):
                make_far(chip, trow, p)
            make_far(chip, other, 0)

        loop(depth - 3, late)
        far_arrival(other, 1)
        make_far(z, other, 1)
        make_far(chip_in, other, 1)
        loop(depth - 3, lambda i: make_far(late_chip(i), other, 1))

    everything = pl.ds(0, trows * strip)

    @pl.when(~edge)
    def _():
        def late(i):
            chip = late_chip(i)
            act(chip, everything)
            back(chip, mine)
            send_strip(chip, trow)

        loop(depth - 2, late)
        for p in range(2):
            col_arrival(1, p)

            def some(i):
                back(i, span(other, p))
                send_term(i, other, p)

            loop(depth, some)

    @pl.when(edge)
    def _():
        def late(i):
            chip = late_chip(i)
            act(chip, everything)
            near(chip, mine)

        loop(depth - 2, late)
        col_arrival(1, 0)
        col_arrival(1, 1, 0, kept)
        back(z, theirs)
        send_strip(z, other)
        near(chip_in, theirs)
        loop(depth - 2, lambda i: near(late_chip(i), theirs))
        for t, p in ((trow, 0), (trow, 1), (other, 0), (other, 1)):
            use_given(chip_in, t, p)
            loop(depth - 2, lambda i: use_given(late_chip(i), t, p))


    def drain(i):
        origin = i * CORES + core
        inside = jnp.where(low, i >= z, i <= z)
        for a in range(2):
            @pl.when(inside & ~edge)
            def _():
                either(a, inner, lambda narrow: arrival(held_block(origin, a, narrow), out_send.at[origin, a]))

            @pl.when((i == z) | ~inside)
            def _():
                arrival(held_block(origin, a, False), in_send.at[origin, a])

            either(a, edge & (i != z),
                   lambda narrow: arrival(held_block(origin, a, narrow), pair_send.at[origin, a]))

    loop(depth, drain)

    @pl.when(edge)
    def _():
        for p in range(2):
            far_own(p).wait_send()
        for copy in edge_cols():
            copy.wait_send()
        far_inward().wait_send()

    @pl.when(~edge)
    def _():
        for copy in inner_cols():
            copy.wait_send()

    @pl.when(inner)
    def _():
        far_across().wait_send()

    for j in range(per):
        total = term[lay * per + j]
        for step in range(1, layers):
            source = lax.rem(lay + step, layers)
            for t in range(2):
                for p in range(2):
                    arrival(got.at[source, j, span(t, p)], term_recv.at[source, j, t, p])
            total = total + got[source, j]
        out[j * block:(j + 1) * block, :] = total.T / width

    def drain_terms(chip, carry):
        for t in range(2):
            for p in range(2):
                @pl.when(chip // per != lay)
                def _():
                    term_copy(chip, t, p).wait_send()

                @pl.when(inner & (chip != z - way))
                def _():
                    made_copy(chip, t, p).wait_send()

        return carry

    lax.fori_loop(0, depth, drain_terms, 0)


def local(sizes, act_rows, back_rows, act_cols, back_cols):
    layers, trows, tcols, pieces, cut, kept = sizes
    depth = tcols // CORES
    held, width = act_rows.shape[1:]
    strip = act_cols.shape[1]
    group = tcols // layers * held
    dma = pltpu.SemaphoreType.DMA
    grams = pltpu.VMEM((depth, trows * strip, CORES * held), jnp.float32)
    return pl.pallas_call(
        functools.partial(kernel, sizes),
        out_shape=jax.ShapeDtypeStruct((group, trows * strip), jnp.float32),
        in_specs=[pl.BlockSpec(memory_space=pl.ANY)] * 4,
        out_specs=pl.BlockSpec(memory_space=pltpu.VMEM),
        scratch_shapes=[
            pltpu.VMEM((2, tcols * held, width), act_rows.dtype),
            pltpu.VMEM((2, trows * strip, width), act_cols.dtype),
            pltpu.VMEM((trows * strip, width - kept), act_cols.dtype),
            grams,
            pltpu.VMEM((layers, depth // layers, trows * strip, CORES * held), jnp.float32),
            grams,
            grams,
            dma((4,)),
            dma((tcols, 2 * pieces)),
            dma((tcols, 2)),
            dma((tcols, 2)),
            dma((tcols, 2)),
            dma((tcols, 2)),
            dma((3, 2)),
            dma((3, 2)),
            dma((4,)),
            dma((2, 2)),
            dma((depth, 2, 2)),
            dma((depth, 2, 2)),
            dma((depth, 2, 2)),
            dma((layers, depth // layers, 2, 2)),
        ],
        compiler_params=pltpu.CompilerParams(
            collective_id=0, has_side_effects=True, vmem_limit_bytes=62 * 1024 * 1024
        ),
    )(act_rows, back_rows, act_cols, back_cols)


def solution(mesh):
    layers, trows, tcols = (mesh.shape[name] for name in ("layer", "trow", "tcol"))
    in_specs = (
        P("layer", ("trow", "tcol"), None),
        P("layer", ("trow", "tcol"), None),
        P("layer", ("tcol", "trow"), None),
        P("layer", ("tcol", "trow"), None),
    )
    out_specs = P(("trow", "layer"), "tcol")

    def body(act_rows, back_rows, act_cols, back_cols):
        held, strip = act_rows.shape[1], act_cols.shape[1]
        pieces = held // GRANULE
        cut = strip // 2
        kept = act_rows.shape[2] * 5 // 16
        return local((layers, trows, tcols, pieces, cut, kept), act_rows, back_rows, act_cols, back_cols)

    return jax.shard_map(body, mesh=mesh, in_specs=in_specs, out_specs=out_specs, check_vma=False)
```

```python
import functools

import jax
import jax.numpy as jnp
from jax import lax
from jax.experimental import pallas as pl
from jax.experimental.pallas import tpu as pltpu
from jax.sharding import PartitionSpec as P

MESH = pl.DeviceIdType.MESH
CORES = 2
GRANULE = 16
AHEAD = 2
TRANS = (((1,), (1,)), ((), ()))


def kernel(sizes, act_rows, back_rows, act_cols, back_cols, out, rows, cols, far, term, got, made, given,
           own_sem, row_recv, mate_recv, in_send, out_send, pair_send, col_send, col_recv, far_send, far_recv,
           made_send, given_recv, term_send, term_recv):
    layers, trows, tcols, pieces, cut, kept = sizes
    depth = tcols // CORES
    per = depth // layers
    held, width = act_rows.shape[1:]
    part = held // pieces
    block = CORES * held
    strip = act_cols.shape[1]
    lay, trow, me = lax.axis_index("layer"), lax.axis_index("trow"), lax.axis_index("tcol")
    z, core = me // CORES, me % CORES
    mate, other = z * CORES + 1 - core, 1 - trow
    own_rows, own_cols = (act_rows, back_rows), (act_cols, back_cols)
    chunks = [(a, h) for h in range(pieces) for a in range(2)]
    low = z < depth // 2
    way = jnp.where(low, 1, -1)
    n_in = jnp.where(low, depth - 1 - z, z)
    n_out = depth - 1 - n_in
    edge, inner, middle = n_out == 0, n_out == 1, n_out > 1
    inwards, outwards = me + way * CORES, me - way * CORES

    own = []
    for a in range(2):
        mine = rows.at[a, pl.ds(pl.multiple_of(me * held, held), held)]
        own.append(pltpu.make_async_copy(own_rows[a].at[0], mine, own_sem.at[a]))
        strips = cols.at[a, pl.ds(pl.multiple_of(trow * strip, strip), strip)]
        own.append(pltpu.make_async_copy(own_cols[a].at[0], strips, own_sem.at[2 + a]))

    barrier = pltpu.get_barrier_semaphore()

    def greet(device):
        pl.semaphore_signal(barrier, inc=1, device_id=device, device_id_type=MESH)

    greet({"trow": other})
    greet({"tcol": inwards})

    @pl.when(~edge)
    def _():
        greet({"tcol": outwards})

    for step in range(1, layers):
        greet({"layer": lax.rem(lay + step, layers)})
    greet({"tcol": mate})
    for copy in own:
        copy.start()
    pl.semaphore_wait(barrier, layers + 2 + jnp.minimum(n_out, 1))

    def remote(src, dst, send, recv, device):
        return pltpu.make_async_remote_copy(
            src_ref=src, dst_ref=dst, send_sem=send, recv_sem=recv, device_id=device, device_id_type=MESH
        )

    def arrival(ref, sem):
        pltpu.make_async_copy(ref, ref, sem).wait()


    def row_block(origin, a, h, narrow):
        span = pl.ds(pl.multiple_of(origin * held + h * part, part), part)
        return rows.at[a, span, pl.ds(0, kept)] if narrow else rows.at[a, span]

    def row_copy(origin, a, h, mine, send, recv, target, narrow):
        dst = row_block(origin, a, h, narrow)
        src = dst
        if mine:
            span = pl.ds(h * part, part)
            src = own_rows[a].at[0, span, pl.ds(0, kept)] if narrow else own_rows[a].at[0, span]
        return remote(src, dst, send.at[origin, a], recv, {"tcol": target})

    def chain_recv(origin, a, h):
        return row_recv.at[origin, a * pieces + h]

    def either(a, narrow, body):
        if a == 0:
            body(False)
        else:
            pl.when(~narrow)(lambda: body(False))
            pl.when(narrow)(lambda: body(True))

    def send_in(origin, a, h, mine):
        row_copy(origin, a, h, mine, in_send, chain_recv(origin, a, h), inwards, False).start()

    def send_out(origin, a, h, mine):
        either(a, inner, lambda narrow: row_copy(
            origin, a, h, mine, out_send, chain_recv(origin, a, h), outwards, narrow).start())

    def send_pair(origin, a, h, mine):
        def send(narrow):
            row_copy(origin, a, h, mine, pair_send, mate_recv.at[origin, a], mate, narrow).start()

        if mine:
            send(False)
        else:
            either(a, edge, send)

    def row_arrival(origin, a, h):
        either(a, edge, lambda narrow: arrival(row_block(origin, a, h, narrow), chain_recv(origin, a, h)))

    def held_block(origin, a, narrow):
        mine = pl.ds(pl.multiple_of(origin * held, held), held)
        return rows.at[a, mine, pl.ds(0, kept)] if narrow else rows.at[a, mine]

    def from_mate(chip):
        origin = chip * CORES + 1 - core
        for a in range(2):
            either(a, edge & (chip != z),
                   lambda narrow: arrival(held_block(origin, a, narrow), mate_recv.at[origin, a]))


    lengths = (cut, strip - cut)

    def span(t, p):
        return pl.ds(pl.multiple_of(t * strip + p * cut, GRANULE), lengths[p])

    def strip_of(t):
        return pl.ds(pl.multiple_of(t * strip, strip), strip)

    def col_copy(a, p, start=0, stop=width, sem=None):
        sem = a if sem is None else sem
        src = own_cols[a].at[0, pl.ds(p * cut, lengths[p]), pl.ds(start, stop - start)]
        dst = cols.at[a, span(trow, p), pl.ds(start, stop - start)]
        return remote(src, dst, col_send.at[sem, p], col_recv.at[sem, p], {"trow": other})

    def col_arrival(a, p, start=0, stop=width, sem=None):
        sem = a if sem is None else sem
        arrival(cols.at[a, span(other, p), pl.ds(start, stop - start)], col_recv.at[sem, p])

    def edge_cols():
        return [col_copy(1, 1, kept, width, 2), col_copy(0, 0), col_copy(0, 1), col_copy(1, 0),
                col_copy(1, 1, 0, kept)]

    def inner_cols():
        return [col_copy(0, 0), col_copy(0, 1), col_copy(1, 0), col_copy(1, 1)]

    def far_own(p):
        src = back_cols.at[0, pl.ds(p * cut, lengths[p]), pl.ds(kept, width - kept)]
        return remote(src, far.at[span(trow, p)], far_send.at[p], far_recv.at[trow, p], {"tcol": inwards})

    def far_inward():
        src = cols.at[1, span(other, 1), pl.ds(kept, width - kept)]
        return remote(src, far.at[span(other, 1)], far_send.at[2], far_recv.at[other, 1], {"tcol": inwards})

    def far_across():
        held_far = far.at[span(trow, 0)]
        return remote(held_far, held_far, far_send.at[3], far_recv.at[trow, 0], {"trow": other})

    def far_arrival(t, p):
        arrival(far.at[span(t, p)], far_recv.at[t, p])


    mine, theirs, everything = strip_of(trow), strip_of(other), pl.ds(0, trows * strip)

    def made_copy(chip, t, p):
        return remote(made.at[chip, span(t, p)], given.at[chip, span(t, p)], made_send.at[chip, t, p],
                      given_recv.at[chip, t, p], {"tcol": outwards})

    def term_copy(chip, t, p):
        j, d = lax.rem(chip, per), chip // per
        return remote(term.at[chip, span(t, p)], got.at[lay, j, span(t, p)], term_send.at[chip, t, p],
                      term_recv.at[lay, j, t, p], {"layer": d})

    def send_term(chip, t, p):
        @pl.when(chip // per != lay)
        def _():
            term_copy(chip, t, p).start()

    def rows_of(a, chip, start, stop):
        return rows[a, pl.ds(pl.multiple_of(chip * block, block), block), start:stop]

    def gram(left, a, chip, start=0, stop=width):
        return lax.dot_general(left, rows_of(a, chip, start, stop), TRANS, preferred_element_type=jnp.float32)

    def act(chip, where):
        term[chip, where, :] = gram(cols[0, where, :], 0, chip)

    def back(chip, where):
        term[chip, where, :] = term[chip, where, :] * gram(cols[1, where, :], 1, chip)

    def near(chip, where):
        made[chip, where, :] = gram(cols[1, where, :kept], 1, chip, 0, kept)

    def make_far(chip, t, p):
        where = span(t, p)
        made[chip, where, :] = gram(far[where, :], 1, chip, kept)
        made_copy(chip, t, p).start()

    def make_far_own(chip):
        made[chip, mine, :] = gram(far[mine, :], 1, chip, kept)
        for p in range(2):
            made_copy(chip, trow, p).start()

    def use_given(chip, t, p):
        where = span(t, p)
        arrival(given.at[chip, where], given_recv.at[chip, t, p])
        term[chip, where, :] = term[chip, where, :] * (made[chip, where, :] + given[chip, where, :])
        send_term(chip, t, p)

    def send_strip(chip, t):
        for p in range(2):
            send_term(chip, t, p)

    def inward_chip(hop):
        return z + way * hop

    def late_chip(i):
        hop = i + 2
        return jnp.where(hop <= n_in, z + way * hop, z - way * (hop - n_in))

    def loop(count, body, start=0):
        def step(i, carry):
            body(i)
            return carry

        lax.fori_loop(start, count, step, 0)


    @pl.when(edge)
    def _():
        for p in range(2):
            far_own(p).start()
        for copy in edge_cols():
            copy.start()

    for a, h in chunks:
        send_in(me, a, h, True)

        @pl.when(~edge)
        def _():
            send_out(me, a, h, True)

    @pl.when(~edge)
    def _():
        inner_cols()[0].start()

    @pl.when(middle)
    def _():
        for copy in inner_cols()[1:]:
            copy.start()

    for a, h in chunks:
        send_pair(me, a, h, True)


    def pass_out(origin, a, h):
        row_arrival(origin, a, h)

        @pl.when(~edge)
        def _():
            send_out(origin, a, h, False)

        send_pair(origin, a, h, False)

    def pass_in(origin, a, h):
        row_arrival(origin, a, h)
        send_in(origin, a, h, False)
        send_pair(origin, a, h, False)

    def edge_chunk(a, h):
        @pl.when(inner)
        def _():
            pass_in(me - way * CORES, a, h)

    def chunk(slot, a, h):
        @pl.when(n_in >= slot)
        def _():
            pass_out(me + way * slot * CORES, a, h)

        @pl.when(n_out >= max(slot, 2))
        def _():
            if slot == 1:
                pass_in(me - way * CORES, a, h)
            else:
                pass_in(me - way * slot * CORES, a, h)

    last = len(chunks) - 1
    chip_in, chip_next = inward_chip(1), inward_chip(2)

    def hook(slot, i):
        if slot == 1 and i == min(2, last):
            @pl.when(inner)
            def _():
                far_arrival(trow, 0)
                far_across().start()
                for copy in inner_cols()[1:]:
                    copy.start()

        if slot == 1 and i == min(4, last):
            @pl.when(edge)
            def _():
                col_arrival(1, 1, kept, width, 2)
                far_inward().start()

        if slot == 1 and i == last:
            for copy in own:
                copy.wait()
            from_mate(z)
            from_mate(chip_in)

            @pl.when(inner)
            def _():
                far_arrival(trow, 1)
                make_far_own(z)
                make_far_own(chip_in)
                far_arrival(other, 0)
                make_far(z, other, 0)
                make_far(chip_in, other, 0)

        if slot == 2 and i == min(1, last):
            act(z, mine)
            act(chip_in, mine)

            @pl.when(~edge)
            def _():
                back(z, mine)
                back(chip_in, mine)
                send_strip(z, trow)
                send_strip(chip_in, trow)

            @pl.when(edge)
            def _():
                back(z, mine)
                near(chip_in, mine)
                send_strip(z, trow)

        if slot == 2 and i == min(4, last):
            for p in range(2):
                col_arrival(0, p)
            act(z, theirs)
            act(chip_in, theirs)

        if slot == 2 and i == min(6, last):
            @pl.when(~edge)
            def _():
                col_arrival(1, 0)
                for chip in (z, chip_in):
                    back(chip, span(other, 0))
                    send_term(chip, other, 0)

        if slot == 3 and i == 0:
            @pl.when(edge)
            def _():
                from_mate(chip_next)
                act(chip_next, everything)
                near(chip_next, mine)

        if slot == 3 and i == min(2, last):
            @pl.when(edge)
            def _():
                for chip in (chip_in, chip_next):
                    for p in range(2):
                        use_given(chip, trow, p)

        if slot == 3 and i == min(5, last):
            @pl.when(edge)
            def _():
                col_arrival(1, 0)
                col_arrival(1, 1, 0, kept)
                back(z, theirs)
                send_strip(z, other)
                for chip in (chip_in, chip_next):
                    near(chip, theirs)
                    use_given(chip, other, 0)

    for slot in range(1, depth):
        for i, (a, h) in enumerate(chunks):
            early = i + AHEAD if slot == 2 else i + AHEAD - len(chunks)
            if slot <= 2 and 0 <= early <= last:
                edge_chunk(*chunks[early])

            chunk(slot, a, h)
            hook(slot, i)

    @pl.when(inner)
    def _():
        def late(i):
            chip = late_chip(i)
            from_mate(chip)
            make_far_own(chip)
            make_far(chip, other, 0)

        loop(depth - 3, late)
        far_arrival(other, 1)
        make_far(z, other, 1)
        make_far(chip_in, other, 1)
        loop(depth - 3, lambda i: make_far(late_chip(i), other, 1))
        from_mate(late_chip(depth - 3))

    @pl.when(middle)
    def _():
        loop(depth - 2, lambda i: from_mate(late_chip(i)))

    @pl.when(~edge)
    def _():
        def late(i):
            chip = late_chip(i)
            act(chip, everything)
            back(chip, mine)
            send_strip(chip, trow)
            back(chip, span(other, 0))
            send_term(chip, other, 0)

        loop(depth - 2, late)
        col_arrival(1, 1)

        def rest(i):
            chip = lax.rem((lay + 1) * per + i, depth)
            back(chip, span(other, 1))
            send_term(chip, other, 1)

        loop(depth, rest)

    @pl.when(edge)
    def _():
        def late(i):
            chip = late_chip(i)
            from_mate(chip)
            act(chip, everything)
            near(chip, everything)

        loop(depth - 2, late, 1)
        for t, p in ((trow, 0), (trow, 1), (other, 0)):
            loop(depth - 2, lambda i: use_given(late_chip(i), t, p), 1)
        for chip in (chip_in, chip_next):
            use_given(chip, other, 1)
        loop(depth - 2, lambda i: use_given(late_chip(i), other, 1), 1)


    def drain(i):
        origin = i * CORES + core
        inside = jnp.where(low, i >= z, i <= z)
        for a in range(2):
            @pl.when(inside & ~edge)
            def _():
                either(a, inner, lambda narrow: arrival(held_block(origin, a, narrow), out_send.at[origin, a]))

            @pl.when((i == z) | ~inside)
            def _():
                arrival(held_block(origin, a, False), in_send.at[origin, a])

            either(a, edge & (i != z),
                   lambda narrow: arrival(held_block(origin, a, narrow), pair_send.at[origin, a]))

    loop(depth, drain)

    @pl.when(edge)
    def _():
        for p in range(2):
            far_own(p).wait_send()
        for copy in edge_cols():
            copy.wait_send()
        far_inward().wait_send()

    @pl.when(~edge)
    def _():
        for copy in inner_cols():
            copy.wait_send()

    @pl.when(inner)
    def _():
        far_across().wait_send()

    for j in range(per):
        total = term[lay * per + j]
        for step in range(1, layers):
            source = lax.rem(lay + step, layers)
            for t in range(2):
                for p in range(2):
                    arrival(got.at[source, j, span(t, p)], term_recv.at[source, j, t, p])
            total = total + got[source, j]
        out[j * block:(j + 1) * block, :] = total.T * (1.0 / width)

    def drain_terms(chip, carry):
        for t in range(2):
            for p in range(2):
                @pl.when(chip // per != lay)
                def _():
                    term_copy(chip, t, p).wait_send()

                @pl.when(inner & (chip != z - way))
                def _():
                    made_copy(chip, t, p).wait_send()

        return carry

    lax.fori_loop(0, depth, drain_terms, 0)


def local(sizes, act_rows, back_rows, act_cols, back_cols):
    layers, trows, tcols, pieces, cut, kept = sizes
    depth = tcols // CORES
    held, width = act_rows.shape[1:]
    strip = act_cols.shape[1]
    group = tcols // layers * held
    dma = pltpu.SemaphoreType.DMA
    grams = pltpu.VMEM((depth, trows * strip, CORES * held), jnp.float32)
    return pl.pallas_call(
        functools.partial(kernel, sizes),
        out_shape=jax.ShapeDtypeStruct((group, trows * strip), jnp.float32),
        in_specs=[pl.BlockSpec(memory_space=pl.ANY)] * 4,
        out_specs=pl.BlockSpec(memory_space=pltpu.VMEM),
        scratch_shapes=[
            pltpu.VMEM((2, tcols * held, width), act_rows.dtype),
            pltpu.VMEM((2, trows * strip, width), act_cols.dtype),
            pltpu.VMEM((trows * strip, width - kept), act_cols.dtype),
            grams,
            pltpu.VMEM((layers, depth // layers, trows * strip, CORES * held), jnp.float32),
            grams,
            grams,
            dma((4,)),
            dma((tcols, 2 * pieces)),
            dma((tcols, 2)),
            dma((tcols, 2)),
            dma((tcols, 2)),
            dma((tcols, 2)),
            dma((3, 2)),
            dma((3, 2)),
            dma((4,)),
            dma((2, 2)),
            dma((depth, 2, 2)),
            dma((depth, 2, 2)),
            dma((depth, 2, 2)),
            dma((layers, depth // layers, 2, 2)),
        ],
        compiler_params=pltpu.CompilerParams(
            collective_id=0, has_side_effects=True, vmem_limit_bytes=62 * 1024 * 1024
        ),
    )(act_rows, back_rows, act_cols, back_cols)


def solution(mesh):
    layers, trows, tcols = (mesh.shape[name] for name in ("layer", "trow", "tcol"))
    in_specs = (
        P("layer", ("trow", "tcol"), None),
        P("layer", ("trow", "tcol"), None),
        P("layer", ("tcol", "trow"), None),
        P("layer", ("tcol", "trow"), None),
    )
    out_specs = P(("trow", "layer"), "tcol")

    def body(act_rows, back_rows, act_cols, back_cols):
        held, strip = act_rows.shape[1], act_cols.shape[1]
        pieces = held // GRANULE
        cut = strip // 2
        kept = act_rows.shape[2] * 5 // 16
        return local((layers, trows, tcols, pieces, cut, kept), act_rows, back_rows, act_cols, back_cols)

    return jax.shard_map(body, mesh=mesh, in_specs=in_specs, out_specs=out_specs, check_vma=False)
```

```python
import functools

import jax
import jax.numpy as jnp
from jax import lax
from jax.experimental import pallas as pl
from jax.experimental.pallas import tpu as pltpu
from jax.sharding import PartitionSpec as P

MESH = pl.DeviceIdType.MESH
CORES = 2
GRANULE = 16
AHEAD = 3
TRANS = (((1,), (1,)), ((), ()))


def kernel(sizes, act_rows, back_rows, act_cols, back_cols, out, rows, cols, far, term, got, made, given,
           own_sem, row_recv, mate_recv, in_send, out_send, pair_send, col_send, col_recv, far_send, far_recv,
           made_send, given_recv, term_send, term_recv):
    layers, trows, tcols, pieces, cut, kept = sizes
    depth = tcols // CORES
    per = depth // layers
    held, width = act_rows.shape[1:]
    part = held // pieces
    block = CORES * held
    strip = act_cols.shape[1]
    lay, trow, me = lax.axis_index("layer"), lax.axis_index("trow"), lax.axis_index("tcol")
    z, core = me // CORES, me % CORES
    mate, other = z * CORES + 1 - core, 1 - trow
    own_rows, own_cols = (act_rows, back_rows), (act_cols, back_cols)
    chunks = [(a, h) for h in range(pieces) for a in range(2)]
    low = z < depth // 2
    way = jnp.where(low, 1, -1)
    n_in = jnp.where(low, depth - 1 - z, z)
    n_out = depth - 1 - n_in
    edge, inner, middle = n_out == 0, n_out == 1, n_out > 1
    inwards, outwards = me + way * CORES, me - way * CORES

    own = []
    for a in range(2):
        mine = rows.at[a, pl.ds(pl.multiple_of(me * held, held), held)]
        own.append(pltpu.make_async_copy(own_rows[a].at[0], mine, own_sem.at[a]))
        strips = cols.at[a, pl.ds(pl.multiple_of(trow * strip, strip), strip)]
        own.append(pltpu.make_async_copy(own_cols[a].at[0], strips, own_sem.at[2 + a]))

    barrier = pltpu.get_barrier_semaphore()

    def greet(device):
        pl.semaphore_signal(barrier, inc=1, device_id=device, device_id_type=MESH)

    greet({"trow": other})
    greet({"tcol": inwards})

    @pl.when(~edge)
    def _():
        greet({"tcol": outwards})

    for step in range(1, layers):
        greet({"layer": lax.rem(lay + step, layers)})
    greet({"tcol": mate})
    for copy in own:
        copy.start()
    pl.semaphore_wait(barrier, layers + 2 + jnp.minimum(n_out, 1))

    def remote(src, dst, send, recv, device):
        return pltpu.make_async_remote_copy(
            src_ref=src, dst_ref=dst, send_sem=send, recv_sem=recv, device_id=device, device_id_type=MESH
        )

    def arrival(ref, sem):
        pltpu.make_async_copy(ref, ref, sem).wait()


    def row_block(origin, a, h, narrow):
        span = pl.ds(pl.multiple_of(origin * held + h * part, part), part)
        return rows.at[a, span, pl.ds(0, kept)] if narrow else rows.at[a, span]

    def row_copy(origin, a, h, mine, send, recv, target, narrow):
        dst = row_block(origin, a, h, narrow)
        src = dst
        if mine:
            span = pl.ds(h * part, part)
            src = own_rows[a].at[0, span, pl.ds(0, kept)] if narrow else own_rows[a].at[0, span]
        return remote(src, dst, send.at[origin, a], recv, {"tcol": target})

    def chain_recv(origin, a, h):
        return row_recv.at[origin, a * pieces + h]

    def either(a, narrow, body):
        if a == 0:
            body(False)
        else:
            pl.when(~narrow)(lambda: body(False))
            pl.when(narrow)(lambda: body(True))

    def send_in(origin, a, h, mine):
        row_copy(origin, a, h, mine, in_send, chain_recv(origin, a, h), inwards, False).start()

    def send_out(origin, a, h, mine):
        either(a, inner, lambda narrow: row_copy(
            origin, a, h, mine, out_send, chain_recv(origin, a, h), outwards, narrow).start())

    def send_pair(origin, a, h, mine):
        def send(narrow):
            row_copy(origin, a, h, mine, pair_send, mate_recv.at[origin, a], mate, narrow).start()

        if mine:
            send(False)
        else:
            either(a, edge, send)

    def row_arrival(origin, a, h):
        either(a, edge, lambda narrow: arrival(row_block(origin, a, h, narrow), chain_recv(origin, a, h)))

    def held_block(origin, a, narrow):
        mine = pl.ds(pl.multiple_of(origin * held, held), held)
        return rows.at[a, mine, pl.ds(0, kept)] if narrow else rows.at[a, mine]

    def from_mate(chip):
        origin = chip * CORES + 1 - core
        for a in range(2):
            either(a, edge & (chip != z),
                   lambda narrow: arrival(held_block(origin, a, narrow), mate_recv.at[origin, a]))


    lengths = (cut, strip - cut)

    def span(t, p):
        return pl.ds(pl.multiple_of(t * strip + p * cut, GRANULE), lengths[p])

    def strip_of(t):
        return pl.ds(pl.multiple_of(t * strip, strip), strip)

    def col_copy(a, p, start=0, stop=width, sem=None):
        sem = a if sem is None else sem
        src = own_cols[a].at[0, pl.ds(p * cut, lengths[p]), pl.ds(start, stop - start)]
        dst = cols.at[a, span(trow, p), pl.ds(start, stop - start)]
        return remote(src, dst, col_send.at[sem, p], col_recv.at[sem, p], {"trow": other})

    def col_arrival(a, p, start=0, stop=width, sem=None):
        sem = a if sem is None else sem
        arrival(cols.at[a, span(other, p), pl.ds(start, stop - start)], col_recv.at[sem, p])

    def edge_cols():
        return [col_copy(1, 1, kept, width, 2), col_copy(0, 0), col_copy(0, 1), col_copy(1, 0),
                col_copy(1, 1, 0, kept)]

    def inner_cols():
        return [col_copy(0, 0), col_copy(0, 1), col_copy(1, 0), col_copy(1, 1, kept, width, 2), col_copy(1, 1, 0, kept)]

    def far_own(p):
        src = back_cols.at[0, pl.ds(p * cut, lengths[p]), pl.ds(kept, width - kept)]
        return remote(src, far.at[span(trow, p)], far_send.at[p], far_recv.at[trow, p], {"tcol": inwards})

    def far_inward():
        src = cols.at[1, span(other, 1), pl.ds(kept, width - kept)]
        return remote(src, far.at[span(other, 1)], far_send.at[2], far_recv.at[other, 1], {"tcol": inwards})

    def far_across():
        held_far = far.at[span(trow, 0)]
        return remote(held_far, held_far, far_send.at[3], far_recv.at[trow, 0], {"trow": other})

    def far_arrival(t, p):
        arrival(far.at[span(t, p)], far_recv.at[t, p])


    mine, theirs, everything = strip_of(trow), strip_of(other), pl.ds(0, trows * strip)

    def made_copy(chip, t, p):
        return remote(made.at[chip, span(t, p)], given.at[chip, span(t, p)], made_send.at[chip, t, p],
                      given_recv.at[chip, t, p], {"tcol": outwards})

    def term_copy(chip, t, p):
        j, d = lax.rem(chip, per), chip // per
        return remote(term.at[chip, span(t, p)], got.at[lay, j, span(t, p)], term_send.at[chip, t, p],
                      term_recv.at[lay, j, t, p], {"layer": d})

    def send_term(chip, t, p):
        @pl.when(chip // per != lay)
        def _():
            term_copy(chip, t, p).start()

    def rows_of(a, chip, start, stop):
        return rows[a, pl.ds(pl.multiple_of(chip * block, block), block), start:stop]

    def gram(left, a, chip, start=0, stop=width):
        return lax.dot_general(left, rows_of(a, chip, start, stop), TRANS, preferred_element_type=jnp.float32)

    def act(chip, where):
        term[chip, where, :] = gram(cols[0, where, :], 0, chip)

    def back(chip, where):
        term[chip, where, :] = term[chip, where, :] * gram(cols[1, where, :], 1, chip)

    def near(chip, where):
        made[chip, where, :] = gram(cols[1, where, :kept], 1, chip, 0, kept)

    def make_far(chip, t, p):
        where = span(t, p)
        made[chip, where, :] = gram(far[where, :], 1, chip, kept)
        made_copy(chip, t, p).start()

    def whole_chip(chip):
        act(chip, everything)
        back(chip, mine)
        send_strip(chip, trow)
        back(chip, span(other, 0))
        send_term(chip, other, 0)

    def last_piece(start, stop):
        left = cols[1, span(other, 1), start:stop]
        return lax.dot_general(left, rows[1, :, start:stop], TRANS, preferred_element_type=jnp.float32)

    def make_far_own(chip):
        made[chip, mine, :] = gram(far[mine, :], 1, chip, kept)
        for p in range(2):
            made_copy(chip, trow, p).start()

    def use_given(chip, t, p):
        where = span(t, p)
        arrival(given.at[chip, where], given_recv.at[chip, t, p])
        term[chip, where, :] = term[chip, where, :] * (made[chip, where, :] + given[chip, where, :])
        send_term(chip, t, p)

    def send_strip(chip, t):
        for p in range(2):
            send_term(chip, t, p)

    def inward_chip(hop):
        return z + way * hop

    def late_chip(i):
        hop = i + 2
        return jnp.where(hop <= n_in, z + way * hop, z - way * (hop - n_in))

    def loop(count, body, start=0):
        def step(i, carry):
            body(i)
            return carry

        lax.fori_loop(start, count, step, 0)


    @pl.when(edge)
    def _():
        for p in range(2):
            far_own(p).start()
        for copy in edge_cols():
            copy.start()

    for a, h in chunks:
        send_in(me, a, h, True)

        @pl.when(~edge)
        def _():
            send_out(me, a, h, True)

    @pl.when(~edge)
    def _():
        inner_cols()[0].start()

    @pl.when(middle)
    def _():
        for copy in inner_cols()[1:]:
            copy.start()

    for a, h in chunks:
        send_pair(me, a, h, True)


    def pass_out(origin, a, h):
        row_arrival(origin, a, h)

        @pl.when(~edge)
        def _():
            send_out(origin, a, h, False)

        send_pair(origin, a, h, False)

    def pass_in(origin, a, h):
        row_arrival(origin, a, h)
        send_in(origin, a, h, False)
        send_pair(origin, a, h, False)

    def edge_chunk(a, h):
        @pl.when(inner)
        def _():
            pass_in(me - way * CORES, a, h)

    def chunk(slot, a, h):
        @pl.when(n_in >= slot)
        def _():
            pass_out(me + way * slot * CORES, a, h)

        @pl.when(n_out >= max(slot, 2))
        def _():
            if slot == 1:
                pass_in(me - way * CORES, a, h)
            else:
                pass_in(me - way * slot * CORES, a, h)

    last = len(chunks) - 1
    chip_in, chip_next = inward_chip(1), inward_chip(2)

    def hook(slot, i):
        if slot == 1 and i == min(2, last):
            @pl.when(inner)
            def _():
                far_arrival(trow, 0)
                far_across().start()
                for copy in inner_cols()[1:]:
                    copy.start()

        if slot == 1 and i == min(4, last):
            @pl.when(edge)
            def _():
                col_arrival(1, 1, kept, width, 2)
                far_inward().start()

        if slot == 1 and i == last:
            for copy in own:
                copy.wait()
            from_mate(z)
            from_mate(chip_in)

            @pl.when(inner)
            def _():
                far_arrival(trow, 1)
                make_far_own(z)
                make_far_own(chip_in)
                far_arrival(other, 0)
                make_far(z, other, 0)
                make_far(chip_in, other, 0)

        if slot == 2 and i == min(1, last):
            act(z, mine)
            act(chip_in, mine)

            @pl.when(~edge)
            def _():
                back(z, mine)
                back(chip_in, mine)
                send_strip(z, trow)
                send_strip(chip_in, trow)

            @pl.when(edge)
            def _():
                back(z, mine)
                near(chip_in, mine)
                send_strip(z, trow)

        if slot == 2 and i == min(4, last):
            for p in range(2):
                col_arrival(0, p)
            act(z, theirs)
            act(chip_in, theirs)

        if slot == 2 and i == min(6, last):
            @pl.when(~edge)
            def _():
                col_arrival(1, 0)
                for chip in (z, chip_in):
                    back(chip, span(other, 0))
                    send_term(chip, other, 0)

            @pl.when(inner)
            def _():
                from_mate(z - way)
                whole_chip(z - way)

        if slot == 3 and i == 0:
            @pl.when(edge)
            def _():
                from_mate(chip_next)
                act(chip_next, everything)
                near(chip_next, mine)

        if slot == 3 and i == min(2, last):
            @pl.when(edge)
            def _():
                for chip in (chip_in, chip_next):
                    for p in range(2):
                        use_given(chip, trow, p)

        if slot == 3 and i == min(5, last):
            @pl.when(edge)
            def _():
                col_arrival(1, 0)
                col_arrival(1, 1, 0, kept)
                back(z, theirs)
                send_strip(z, other)
                for chip in (chip_in, chip_next):
                    near(chip, theirs)
                    use_given(chip, other, 0)

    for slot in range(1, depth):
        for i, (a, h) in enumerate(chunks):
            early = i + AHEAD if slot == 2 else i + AHEAD - len(chunks)
            if slot <= 2 and 0 <= early <= last:
                edge_chunk(*chunks[early])

            chunk(slot, a, h)
            hook(slot, i)

    @pl.when(inner)
    def _():
        def late(i):
            chip = late_chip(i)
            from_mate(chip)
            make_far_own(chip)
            make_far(chip, other, 0)

        loop(depth - 3, late)
        far_arrival(other, 1)
        make_far(z, other, 1)
        make_far(chip_in, other, 1)
        loop(depth - 3, lambda i: make_far(late_chip(i), other, 1))
        loop(depth - 3, lambda i: whole_chip(late_chip(i)))

    @pl.when(middle)
    def _():
        loop(depth - 2, lambda i: from_mate(late_chip(i)))
        loop(depth - 2, lambda i: whole_chip(late_chip(i)))

    @pl.when(~edge)
    def _():
        where = span(other, 1)
        col_arrival(1, 1, kept, width, 2)
        first = last_piece(kept, width)
        for chip in range(depth):
            given[chip, where, :] = first[:, chip * block:(chip + 1) * block]
        col_arrival(1, 1, 0, kept)
        second = last_piece(0, kept)
        for chip in range(depth):
            both = given[chip, where, :] + second[:, chip * block:(chip + 1) * block]
            term[chip, where, :] = term[chip, where, :] * both
            send_term(chip, other, 1)

    @pl.when(edge)
    def _():
        def late(i):
            chip = late_chip(i)
            from_mate(chip)
            act(chip, everything)
            near(chip, everything)

        loop(depth - 2, late, 1)
        for t, p in ((trow, 0), (trow, 1), (other, 0)):
            loop(depth - 2, lambda i: use_given(late_chip(i), t, p), 1)
        for chip in (chip_in, chip_next):
            use_given(chip, other, 1)
        loop(depth - 2, lambda i: use_given(late_chip(i), other, 1), 1)


    def drain(i):
        origin = i * CORES + core
        inside = jnp.where(low, i >= z, i <= z)
        for a in range(2):
            @pl.when(inside & ~edge)
            def _():
                either(a, inner, lambda narrow: arrival(held_block(origin, a, narrow), out_send.at[origin, a]))

            @pl.when((i == z) | ~inside)
            def _():
                arrival(held_block(origin, a, False), in_send.at[origin, a])

            either(a, edge & (i != z),
                   lambda narrow: arrival(held_block(origin, a, narrow), pair_send.at[origin, a]))

    loop(depth, drain)

    @pl.when(edge)
    def _():
        for p in range(2):
            far_own(p).wait_send()
        for copy in edge_cols():
            copy.wait_send()
        far_inward().wait_send()

    @pl.when(~edge)
    def _():
        for copy in inner_cols():
            copy.wait_send()

    @pl.when(inner)
    def _():
        far_across().wait_send()

    for j in range(per):
        total = term[lay * per + j]
        for step in range(1, layers):
            source = lax.rem(lay + step, layers)
            for t in range(2):
                for p in range(2):
                    arrival(got.at[source, j, span(t, p)], term_recv.at[source, j, t, p])
            total = total + got[source, j]
        out[j * block:(j + 1) * block, :] = total.T * (1.0 / width)

    def drain_terms(chip, carry):
        for t in range(2):
            for p in range(2):
                @pl.when(chip // per != lay)
                def _():
                    term_copy(chip, t, p).wait_send()

                @pl.when(inner & (chip != z - way))
                def _():
                    made_copy(chip, t, p).wait_send()

        return carry

    lax.fori_loop(0, depth, drain_terms, 0)


def local(sizes, act_rows, back_rows, act_cols, back_cols):
    layers, trows, tcols, pieces, cut, kept = sizes
    depth = tcols // CORES
    held, width = act_rows.shape[1:]
    strip = act_cols.shape[1]
    group = tcols // layers * held
    dma = pltpu.SemaphoreType.DMA
    grams = pltpu.VMEM((depth, trows * strip, CORES * held), jnp.float32)
    return pl.pallas_call(
        functools.partial(kernel, sizes),
        out_shape=jax.ShapeDtypeStruct((group, trows * strip), jnp.float32),
        in_specs=[pl.BlockSpec(memory_space=pl.ANY)] * 4,
        out_specs=pl.BlockSpec(memory_space=pltpu.VMEM),
        scratch_shapes=[
            pltpu.VMEM((2, tcols * held, width), act_rows.dtype),
            pltpu.VMEM((2, trows * strip, width), act_cols.dtype),
            pltpu.VMEM((trows * strip, width - kept), act_cols.dtype),
            grams,
            pltpu.VMEM((layers, depth // layers, trows * strip, CORES * held), jnp.float32),
            grams,
            grams,
            dma((4,)),
            dma((tcols, 2 * pieces)),
            dma((tcols, 2)),
            dma((tcols, 2)),
            dma((tcols, 2)),
            dma((tcols, 2)),
            dma((3, 2)),
            dma((3, 2)),
            dma((4,)),
            dma((2, 2)),
            dma((depth, 2, 2)),
            dma((depth, 2, 2)),
            dma((depth, 2, 2)),
            dma((layers, depth // layers, 2, 2)),
        ],
        compiler_params=pltpu.CompilerParams(
            collective_id=0, has_side_effects=True, vmem_limit_bytes=62 * 1024 * 1024
        ),
    )(act_rows, back_rows, act_cols, back_cols)


def solution(mesh):
    layers, trows, tcols = (mesh.shape[name] for name in ("layer", "trow", "tcol"))
    in_specs = (
        P("layer", ("trow", "tcol"), None),
        P("layer", ("trow", "tcol"), None),
        P("layer", ("tcol", "trow"), None),
        P("layer", ("tcol", "trow"), None),
    )
    out_specs = P(("trow", "layer"), "tcol")

    def body(act_rows, back_rows, act_cols, back_cols):
        held, strip = act_rows.shape[1], act_cols.shape[1]
        pieces = held // GRANULE
        cut = strip // 2
        kept = act_rows.shape[2] * 5 // 16
        return local((layers, trows, tcols, pieces, cut, kept), act_rows, back_rows, act_cols, back_cols)

    return jax.shard_map(body, mesh=mesh, in_specs=in_specs, out_specs=out_specs, check_vma=False)
```

```python
import functools

import jax
import jax.numpy as jnp
from jax import lax
from jax.experimental import pallas as pl
from jax.experimental.pallas import tpu as pltpu
from jax.sharding import PartitionSpec as P

MESH = pl.DeviceIdType.MESH
CORES = 2
GRANULE = 16
AHEAD = 3
TRANS = (((1,), (1,)), ((), ()))


def kernel(sizes, act_rows, back_rows, act_cols, back_cols, out, rows, cols, far, term, got, made, given,
           own_sem, row_recv, mate_recv, in_send, out_send, pair_send, col_send, col_recv, far_send, far_recv,
           made_send, given_recv, term_send, term_recv):
    layers, trows, tcols, pieces, cut, kept = sizes
    depth = tcols // CORES
    per = depth // layers
    held, width = act_rows.shape[1:]
    part = held // pieces
    block = CORES * held
    strip = act_cols.shape[1]
    lay, trow, me = lax.axis_index("layer"), lax.axis_index("trow"), lax.axis_index("tcol")
    z, core = me // CORES, me % CORES
    mate, other = z * CORES + 1 - core, 1 - trow
    own_rows, own_cols = (act_rows, back_rows), (act_cols, back_cols)
    chunks = [(a, h) for h in range(pieces) for a in range(2)]
    low = z < depth // 2
    way = jnp.where(low, 1, -1)
    n_in = jnp.where(low, depth - 1 - z, z)
    n_out = depth - 1 - n_in
    edge, inner, middle = n_out == 0, n_out == 1, n_out > 1
    inwards, outwards = me + way * CORES, me - way * CORES

    own = []
    for a in range(2):
        mine = rows.at[a, pl.ds(pl.multiple_of(me * held, held), held)]
        own.append(pltpu.make_async_copy(own_rows[a].at[0], mine, own_sem.at[a]))
        strips = cols.at[a, pl.ds(pl.multiple_of(trow * strip, strip), strip)]
        own.append(pltpu.make_async_copy(own_cols[a].at[0], strips, own_sem.at[2 + a]))

    barrier = pltpu.get_barrier_semaphore()

    def greet(device):
        pl.semaphore_signal(barrier, inc=1, device_id=device, device_id_type=MESH)

    greet({"trow": other})
    greet({"tcol": inwards})

    @pl.when(~edge)
    def _():
        greet({"tcol": outwards})

    for step in range(1, layers):
        greet({"layer": lax.rem(lay + step, layers)})
    greet({"tcol": mate})
    for copy in own:
        copy.start()
    pl.semaphore_wait(barrier, layers + 2 + jnp.minimum(n_out, 1))

    def remote(src, dst, send, recv, device):
        return pltpu.make_async_remote_copy(
            src_ref=src, dst_ref=dst, send_sem=send, recv_sem=recv, device_id=device, device_id_type=MESH
        )

    def arrival(ref, sem):
        pltpu.make_async_copy(ref, ref, sem).wait()


    def row_block(origin, a, h, narrow):
        span = pl.ds(pl.multiple_of(origin * held + h * part, part), part)
        return rows.at[a, span, pl.ds(0, kept)] if narrow else rows.at[a, span]

    def row_copy(origin, a, h, mine, send, recv, target, narrow):
        dst = row_block(origin, a, h, narrow)
        src = dst
        if mine:
            span = pl.ds(h * part, part)
            src = own_rows[a].at[0, span, pl.ds(0, kept)] if narrow else own_rows[a].at[0, span]
        return remote(src, dst, send.at[origin, a], recv, {"tcol": target})

    def chain_recv(origin, a, h):
        return row_recv.at[origin, a * pieces + h]

    def either(a, narrow, body):
        if a == 0:
            body(False)
        else:
            pl.when(~narrow)(lambda: body(False))
            pl.when(narrow)(lambda: body(True))

    def send_in(origin, a, h, mine):
        row_copy(origin, a, h, mine, in_send, chain_recv(origin, a, h), inwards, False).start()

    def send_out(origin, a, h, mine):
        either(a, inner, lambda narrow: row_copy(
            origin, a, h, mine, out_send, chain_recv(origin, a, h), outwards, narrow).start())

    def send_pair(origin, a, h, mine):
        def send(narrow):
            row_copy(origin, a, h, mine, pair_send, mate_recv.at[origin, a], mate, narrow).start()

        if mine:
            send(False)
        else:
            either(a, edge, send)

    def row_arrival(origin, a, h):
        either(a, edge, lambda narrow: arrival(row_block(origin, a, h, narrow), chain_recv(origin, a, h)))

    def held_block(origin, a, narrow):
        mine = pl.ds(pl.multiple_of(origin * held, held), held)
        return rows.at[a, mine, pl.ds(0, kept)] if narrow else rows.at[a, mine]

    def from_mate(chip):
        origin = chip * CORES + 1 - core
        for a in range(2):
            either(a, edge & (chip != z),
                   lambda narrow: arrival(held_block(origin, a, narrow), mate_recv.at[origin, a]))


    lengths = (cut, strip - cut)

    def span(t, p):
        return pl.ds(pl.multiple_of(t * strip + p * cut, GRANULE), lengths[p])

    def strip_of(t):
        return pl.ds(pl.multiple_of(t * strip, strip), strip)

    def col_copy(a, p, start=0, stop=width, sem=None):
        sem = a if sem is None else sem
        src = own_cols[a].at[0, pl.ds(p * cut, lengths[p]), pl.ds(start, stop - start)]
        dst = cols.at[a, span(trow, p), pl.ds(start, stop - start)]
        return remote(src, dst, col_send.at[sem, p], col_recv.at[sem, p], {"trow": other})

    def col_arrival(a, p, start=0, stop=width, sem=None):
        sem = a if sem is None else sem
        arrival(cols.at[a, span(other, p), pl.ds(start, stop - start)], col_recv.at[sem, p])

    def edge_cols():
        return [col_copy(1, 1, kept, width, 2), col_copy(0, 0), col_copy(0, 1), col_copy(1, 0),
                col_copy(1, 1, 0, kept)]

    def inner_cols():
        return [col_copy(0, 0), col_copy(0, 1), col_copy(1, 0), col_copy(1, 1, kept, width, 2), col_copy(1, 1, 0, kept)]

    def far_own(p):
        src = back_cols.at[0, pl.ds(p * cut, lengths[p]), pl.ds(kept, width - kept)]
        return remote(src, far.at[span(trow, p)], far_send.at[p], far_recv.at[trow, p], {"tcol": inwards})

    def far_inward():
        src = cols.at[1, span(other, 1), pl.ds(kept, width - kept)]
        return remote(src, far.at[span(other, 1)], far_send.at[2], far_recv.at[other, 1], {"tcol": inwards})

    def far_across():
        held_far = far.at[span(trow, 0)]
        return remote(held_far, held_far, far_send.at[3], far_recv.at[trow, 0], {"trow": other})

    def far_arrival(t, p):
        arrival(far.at[span(t, p)], far_recv.at[t, p])


    mine, theirs, everything = strip_of(trow), strip_of(other), pl.ds(0, trows * strip)

    def made_copy(chip, t, p):
        return remote(made.at[chip, span(t, p)], given.at[chip, span(t, p)], made_send.at[chip, t, p],
                      given_recv.at[chip, t, p], {"tcol": outwards})

    def term_copy(chip, t, p):
        j, d = lax.rem(chip, per), chip // per
        return remote(term.at[chip, span(t, p)], got.at[lay, j, span(t, p)], term_send.at[chip, t, p],
                      term_recv.at[lay, j, t, p], {"layer": d})

    def send_term(chip, t, p):
        @pl.when(chip // per != lay)
        def _():
            term_copy(chip, t, p).start()

    def rows_of(a, chip, start, stop):
        return rows[a, pl.ds(pl.multiple_of(chip * block, block), block), start:stop]

    def gram(left, a, chip, start=0, stop=width):
        return lax.dot_general(left, rows_of(a, chip, start, stop), TRANS, preferred_element_type=jnp.float32)

    def act(chip, where):
        term[chip, where, :] = gram(cols[0, where, :], 0, chip)

    def back(chip, where):
        term[chip, where, :] = term[chip, where, :] * gram(cols[1, where, :], 1, chip)

    def near(chip, where):
        made[chip, where, :] = gram(cols[1, where, :kept], 1, chip, 0, kept)

    def make_far(chip, t, p):
        where = span(t, p)
        made[chip, where, :] = gram(far[where, :], 1, chip, kept)
        made_copy(chip, t, p).start()

    def whole_chip(chip):
        act(chip, everything)
        back(chip, mine)
        send_strip(chip, trow)
        back(chip, span(other, 0))
        send_term(chip, other, 0)

    def last_piece(start, stop):
        left = cols[1, span(other, 1), start:stop]
        return lax.dot_general(left, rows[1, :, start:stop], TRANS, preferred_element_type=jnp.float32)

    def make_far_own(chip):
        made[chip, mine, :] = gram(far[mine, :], 1, chip, kept)
        for p in range(2):
            made_copy(chip, trow, p).start()

    def use_given(chip, t, p):
        where = span(t, p)
        arrival(given.at[chip, where], given_recv.at[chip, t, p])
        term[chip, where, :] = term[chip, where, :] * (made[chip, where, :] + given[chip, where, :])
        send_term(chip, t, p)

    def send_strip(chip, t):
        for p in range(2):
            send_term(chip, t, p)

    def inward_chip(hop):
        return z + way * hop

    def late_chip(i):
        hop = i + 2
        return jnp.where(hop <= n_in, z + way * hop, z - way * (hop - n_in))

    def loop(count, body, start=0):
        def step(i, carry):
            body(i)
            return carry

        lax.fori_loop(start, count, step, 0)


    @pl.when(edge)
    def _():
        for p in range(2):
            far_own(p).start()
        for copy in edge_cols():
            copy.start()

    for a, h in chunks:
        send_in(me, a, h, True)

        @pl.when(~edge)
        def _():
            send_out(me, a, h, True)

    @pl.when(~edge)
    def _():
        inner_cols()[0].start()

    @pl.when(middle)
    def _():
        for copy in inner_cols()[1:]:
            copy.start()

    for a, h in chunks:
        send_pair(me, a, h, True)


    def pass_out(origin, a, h):
        row_arrival(origin, a, h)

        @pl.when(~edge)
        def _():
            send_out(origin, a, h, False)

        send_pair(origin, a, h, False)

    def pass_in(origin, a, h):
        row_arrival(origin, a, h)
        send_in(origin, a, h, False)
        send_pair(origin, a, h, False)

    def edge_chunk(a, h):
        @pl.when(inner)
        def _():
            pass_in(me - way * CORES, a, h)

    def chunk(slot, a, h):
        @pl.when(n_in >= slot)
        def _():
            pass_out(me + way * slot * CORES, a, h)

        @pl.when(n_out >= max(slot, 2))
        def _():
            if slot == 1:
                pass_in(me - way * CORES, a, h)
            else:
                pass_in(me - way * slot * CORES, a, h)

    last = len(chunks) - 1
    chip_in, chip_next = inward_chip(1), inward_chip(2)

    def hook(slot, i):
        if slot == 1 and i == min(1, last):
            @pl.when(inner)
            def _():
                far_arrival(trow, 0)
                far_across().start()
                for copy in inner_cols()[1:]:
                    copy.start()

        if slot == 1 and i == min(4, last):
            @pl.when(edge)
            def _():
                col_arrival(1, 1, kept, width, 2)
                far_inward().start()

        if slot == 1 and i == last:
            for copy in own:
                copy.wait()
            from_mate(z)
            from_mate(chip_in)

            @pl.when(inner)
            def _():
                far_arrival(trow, 1)
                make_far_own(z)
                make_far_own(chip_in)
                far_arrival(other, 0)
                make_far(z, other, 0)
                make_far(chip_in, other, 0)

        if slot == 2 and i == min(2, last):
            act(z, mine)
            act(chip_in, mine)

            @pl.when(~edge)
            def _():
                back(z, mine)
                back(chip_in, mine)
                send_strip(z, trow)
                send_strip(chip_in, trow)

            @pl.when(edge)
            def _():
                back(z, mine)
                near(chip_in, mine)
                send_strip(z, trow)

        if slot == 2 and i == min(4, last):
            for p in range(2):
                col_arrival(0, p)
            act(z, theirs)
            act(chip_in, theirs)

        if slot == 2 and i == min(6, last):
            @pl.when(~edge)
            def _():
                col_arrival(1, 0)
                for chip in (z, chip_in):
                    back(chip, span(other, 0))
                    send_term(chip, other, 0)

            @pl.when(inner)
            def _():
                from_mate(z - way)
                whole_chip(z - way)

        if slot == 3 and i == 0:
            @pl.when(edge)
            def _():
                from_mate(chip_next)
                act(chip_next, everything)
                near(chip_next, mine)

        if slot == 3 and i == min(2, last):
            @pl.when(edge)
            def _():
                for chip in (chip_in, chip_next):
                    for p in range(2):
                        use_given(chip, trow, p)

        if slot == 3 and i == min(5, last):
            @pl.when(edge)
            def _():
                col_arrival(1, 0)
                col_arrival(1, 1, 0, kept)
                back(z, theirs)
                send_strip(z, other)
                for chip in (chip_in, chip_next):
                    near(chip, theirs)
                    use_given(chip, other, 0)

    for slot in range(1, depth):
        for i, (a, h) in enumerate(chunks):
            early = i + AHEAD if slot == 2 else i + AHEAD - len(chunks)
            if slot <= 2 and 0 <= early <= last:
                edge_chunk(*chunks[early])

            chunk(slot, a, h)
            hook(slot, i)

    @pl.when(inner)
    def _():
        def late(i):
            chip = late_chip(i)
            from_mate(chip)
            make_far_own(chip)
            make_far(chip, other, 0)

        loop(depth - 3, late)
        far_arrival(other, 1)
        make_far(z, other, 1)
        make_far(chip_in, other, 1)
        loop(depth - 3, lambda i: make_far(late_chip(i), other, 1))
        loop(depth - 3, lambda i: whole_chip(late_chip(i)))

    @pl.when(middle)
    def _():
        loop(depth - 2, lambda i: from_mate(late_chip(i)))
        loop(depth - 2, lambda i: whole_chip(late_chip(i)))

    @pl.when(~edge)
    def _():
        where = span(other, 1)
        col_arrival(1, 1, kept, width, 2)
        first = last_piece(kept, width)
        for chip in range(depth):
            given[chip, where, :] = first[:, chip * block:(chip + 1) * block]
        col_arrival(1, 1, 0, kept)
        second = last_piece(0, kept)
        for chip in range(depth):
            both = given[chip, where, :] + second[:, chip * block:(chip + 1) * block]
            term[chip, where, :] = term[chip, where, :] * both
            send_term(chip, other, 1)

    @pl.when(edge)
    def _():
        def late(i):
            chip = late_chip(i)
            from_mate(chip)
            act(chip, everything)
            near(chip, everything)

        loop(depth - 2, late, 1)
        for t, p in ((trow, 0), (trow, 1), (other, 0)):
            loop(depth - 2, lambda i: use_given(late_chip(i), t, p), 1)
        for chip in (chip_in, chip_next):
            use_given(chip, other, 1)
        loop(depth - 2, lambda i: use_given(late_chip(i), other, 1), 1)


    def drain(i):
        origin = i * CORES + core
        inside = jnp.where(low, i >= z, i <= z)
        for a in range(2):
            @pl.when(inside & ~edge)
            def _():
                either(a, inner, lambda narrow: arrival(held_block(origin, a, narrow), out_send.at[origin, a]))

            @pl.when((i == z) | ~inside)
            def _():
                arrival(held_block(origin, a, False), in_send.at[origin, a])

            either(a, edge & (i != z),
                   lambda narrow: arrival(held_block(origin, a, narrow), pair_send.at[origin, a]))

    loop(depth, drain)

    @pl.when(edge)
    def _():
        for p in range(2):
            far_own(p).wait_send()
        for copy in edge_cols():
            copy.wait_send()
        far_inward().wait_send()

    @pl.when(~edge)
    def _():
        for copy in inner_cols():
            copy.wait_send()

    @pl.when(inner)
    def _():
        far_across().wait_send()

    for j in range(per):
        total = term[lay * per + j]
        for step in range(1, layers):
            source = lax.rem(lay + step, layers)
            for t in range(2):
                for p in range(2):
                    arrival(got.at[source, j, span(t, p)], term_recv.at[source, j, t, p])
            total = total + got[source, j]
        out[j * block:(j + 1) * block, :] = total.T * (1.0 / width)

    def drain_terms(chip, carry):
        for t in range(2):
            for p in range(2):
                @pl.when(chip // per != lay)
                def _():
                    term_copy(chip, t, p).wait_send()

                @pl.when(inner & (chip != z - way))
                def _():
                    made_copy(chip, t, p).wait_send()

        return carry

    lax.fori_loop(0, depth, drain_terms, 0)


def local(sizes, act_rows, back_rows, act_cols, back_cols):
    layers, trows, tcols, pieces, cut, kept = sizes
    depth = tcols // CORES
    held, width = act_rows.shape[1:]
    strip = act_cols.shape[1]
    group = tcols // layers * held
    dma = pltpu.SemaphoreType.DMA
    grams = pltpu.VMEM((depth, trows * strip, CORES * held), jnp.float32)
    return pl.pallas_call(
        functools.partial(kernel, sizes),
        out_shape=jax.ShapeDtypeStruct((group, trows * strip), jnp.float32),
        in_specs=[pl.BlockSpec(memory_space=pl.ANY)] * 4,
        out_specs=pl.BlockSpec(memory_space=pltpu.VMEM),
        scratch_shapes=[
            pltpu.VMEM((2, tcols * held, width), act_rows.dtype),
            pltpu.VMEM((2, trows * strip, width), act_cols.dtype),
            pltpu.VMEM((trows * strip, width - kept), act_cols.dtype),
            grams,
            pltpu.VMEM((layers, depth // layers, trows * strip, CORES * held), jnp.float32),
            grams,
            grams,
            dma((4,)),
            dma((tcols, 2 * pieces)),
            dma((tcols, 2)),
            dma((tcols, 2)),
            dma((tcols, 2)),
            dma((tcols, 2)),
            dma((3, 2)),
            dma((3, 2)),
            dma((4,)),
            dma((2, 2)),
            dma((depth, 2, 2)),
            dma((depth, 2, 2)),
            dma((depth, 2, 2)),
            dma((layers, depth // layers, 2, 2)),
        ],
        compiler_params=pltpu.CompilerParams(
            collective_id=0, has_side_effects=True, vmem_limit_bytes=62 * 1024 * 1024
        ),
    )(act_rows, back_rows, act_cols, back_cols)


def solution(mesh):
    layers, trows, tcols = (mesh.shape[name] for name in ("layer", "trow", "tcol"))
    in_specs = (
        P("layer", ("trow", "tcol"), None),
        P("layer", ("trow", "tcol"), None),
        P("layer", ("tcol", "trow"), None),
        P("layer", ("tcol", "trow"), None),
    )
    out_specs = P(("trow", "layer"), "tcol")

    def body(act_rows, back_rows, act_cols, back_cols):
        held, strip = act_rows.shape[1], act_cols.shape[1]
        pieces = held // GRANULE
        cut = strip // 2
        kept = act_rows.shape[2] * 5 // 16
        return local((layers, trows, tcols, pieces, cut, kept), act_rows, back_rows, act_cols, back_cols)

    return jax.shard_map(body, mesh=mesh, in_specs=in_specs, out_specs=out_specs, check_vma=False)
```
